32 devices in a mesh: row: 8 (over y, x, core), col: 4 (over z).
Axes of the slice: x: 2, y: 2, z: 4, core: 2. Of those that a mesh axis runs over, the one named last changes fastest.
Arguments:
- inverse_tiles: float32 [512, 512], P('row', 'col'), may hold values from -0.375 to 0.375
- factor_panels: float32 [3, 512, 256], P(None, 'row', 'col'), may hold values from -6 to 6
- block_rows: int32 [3, 8], replicated, may hold values from 0 to 15, as said below
- couplings: float32 [2, 512, 512], replicated, may hold values from -0.25 to 0.25
Outputs:
- new_columns: float32 [3, 512, 512], P(None, ('row', 'col'))
The draws below stay inside these ranges and needn't reach their ends.
Inputs may be any that keep to these rules, and one draw needn't show every extreme that they name: `block_rows`: each row lists 8 different row blocks in no particular order; in each row, all 4 blocks q * 4 to q * 4 + 3 of some q are listed.
All inputs are finite; a program needn't handle non-finite values.
Results may differ from the reference program's by a relative error of at most 0.0001.
Values sent between devices are 32-bit elements; how exact they have to be, the bound alone decides.
No kernel may reach another device: no remote copies, remote signals or barrier semaphores. Data moves between devices by JAX's collectives and lax.ppermute only.
A program may use at most 64 MiB of HBM per device.

```python
import jax
import jax.numpy as jnp
from jax import lax

W = 512
RB = 32
SUPERNODES = 3
M = 512
NB = 16
NBC = 4
NZB = 8
NZ = 256


def draw_block_rows(key, part):
    listed = []
    for section in range(SUPERNODES):
        branch = jax.random.fold_in(key, 11 + section)
        order = jax.random.permutation(jax.random.fold_in(branch, 1), NB).astype(jnp.int32)
        chosen = jax.random.randint(jax.random.fold_in(branch, 2), (), 0, NB // NBC)
        blocks = jnp.arange(NB, dtype=jnp.int32)
        scores = order + NB * (blocks // NBC == chosen).astype(jnp.int32)
        picked = lax.top_k(scores, NZB)[1].astype(jnp.int32)
        listed.append(jax.random.permutation(jax.random.fold_in(branch, 3), picked))
    return jnp.stack(listed).astype(jnp.int32)


def levels(own_key, shape, shards, least, top_value):
    loudness = 1.0
    for axis_at, blocks in shards:
        draws = jax.random.uniform(jax.random.fold_in(jax.random.fold_in(own_key, 6), axis_at), (blocks,), jnp.float32, least / len(shards), top_value / len(shards))
        loudness = loudness * jnp.repeat(jnp.exp(draws), shape[axis_at] // blocks).reshape((-1,) + (1,) * (len(shape) - 1 - axis_at))
    return loudness


def gaussian(key, extent, deviation, most, cuts=(), kind=jnp.bfloat16):
    array = deviation * jax.random.normal(key, extent, jnp.float32)
    if cuts:
        array = array * levels(key, extent, cuts, -0.22, 0.18)
    return jnp.clip(array, -most, most).astype(kind)


def setup_inputs(seed: int = 0) -> dict:
    key_of = jax.random.split(jax.random.key(seed), 5)
    return {
        "inverse_tiles": gaussian(key_of[0], (M, M), NZ ** -0.5, 0.375, ((0, 8), (1, 4)), jnp.float32),
        "factor_panels": gaussian(key_of[1], (SUPERNODES, W, NZ), 1.0, 6.0, ((1, 8), (2, 4)), jnp.float32),
        "block_rows": draw_block_rows(jax.random.fold_in(key_of[4], 71), 0),
        "couplings": gaussian(key_of[3], (SUPERNODES - 1, W, W), W ** -0.5, 0.25, (), jnp.float32),
    }


def reference(inverse_tiles, factor_panels, block_rows, couplings):
    results = []
    previous = None
    for section in range(SUPERNODES):
        onehot = (block_rows[section][:, None] == jnp.arange(NB, dtype=jnp.int32)[None, :]).astype(jnp.float32)
        blocks = factor_panels[section].reshape(W, NZB, RB)
        full_t = jnp.einsum("wpr,pb->wbr", blocks, onehot, precision=lax.Precision.HIGHEST).reshape(W, M)
        product = lax.dot_general(inverse_tiles, full_t, (((1,), (1,)), ((), ())), precision=lax.Precision.HIGHEST, preferred_element_type=jnp.float32)
        if previous is not None:
            product = product + jnp.dot(previous, couplings[section - 1], precision=lax.Precision.HIGHEST, preferred_element_type=jnp.float32)
        previous = -product
        results.append(previous)
    return jnp.stack(results)
```

```python
import functools

import jax
import jax.numpy as jnp
from jax import lax
from jax.experimental import pallas as pl
from jax.experimental.pallas import tpu as pltpu
from jax.sharding import PartitionSpec as P

LANES = 128
CORES = 2
REPLICA_BYTES = 4 << 20
KERNEL_BYTES = 12 << 20
VMEM = pl.BlockSpec(memory_space=pltpu.VMEM)
SMEM = pl.BlockSpec(memory_space=pltpu.SMEM)


def streamed(inverse_tiles, factor_panels, block_rows, couplings):
    tile_rows, tile_cols = inverse_tiles.shape
    piece_rows = factor_panels.shape[1]
    listed = block_rows.shape[1]
    col_count = lax.axis_size("col")
    block_size = factor_panels.shape[2] * col_count // listed
    local_blocks = tile_cols // block_size
    my_column = lax.axis_index("col")
    offset = my_column * local_blocks
    targets = offset + jnp.arange(local_blocks, dtype=jnp.int32)
    results = []
    previous = None
    for section in range(factor_panels.shape[0]):
        section_rows = block_rows[section]
        gathered = lax.all_gather(factor_panels[section], "col", axis=1, tiled=True)
        onehot = (section_rows[:, None] == targets[None, :]).astype(jnp.float32)
        picked = jnp.einsum(
            "wpr,pq->wqr",
            gathered.reshape(piece_rows, listed, block_size),
            onehot,
            precision=lax.Precision.HIGHEST,
        ).reshape(piece_rows, tile_cols)
        partial_value = lax.dot_general(
            inverse_tiles,
            lax.all_gather(picked, "row", axis=0, tiled=True),
            (((1,), (1,)), ((), ())),
            precision=lax.Precision.HIGHEST,
            preferred_element_type=jnp.float32,
        )
        summed = lax.psum_scatter(partial_value, "col", scatter_dimension=0, tiled=True)
        if previous is not None:
            summed = summed + jnp.dot(
                previous,
                couplings[section - 1],
                precision=lax.Precision.HIGHEST,
                preferred_element_type=jnp.float32,
            )
        previous = -summed
        results.append(previous)
    return jnp.stack(results)


def call(kernel, out_shape, specs, name, scratch=()):
    return pl.pallas_call(
        kernel,
        out_shape=out_shape,
        in_specs=specs,
        out_specs=jax.tree.map(lambda _: VMEM, out_shape),
        scratch_shapes=scratch,
        compiler_params=pltpu.CompilerParams(vmem_limit_bytes=KERNEL_BYTES),
        name=name,
    )


def split(value):
    high = value.astype(jnp.bfloat16)
    return high, (value - high.astype(jnp.float32)).astype(jnp.bfloat16)


def swap(value, axis, distance):
    count = lax.axis_size(axis)
    return lax.ppermute(value, axis, [(i, i ^ distance) for i in range(count)])


def pack_kernel(rows, fold, tile_ref, panel_ref, *outs):
    column = lax.axis_index("col")
    high = panel_ref.shape[1] // fold
    for section in range(panel_ref.shape[0]):
        dense = jnp.concatenate(
            [panel_ref[section, i * high : (i + 1) * high, :] for i in range(fold)], axis=1
        )
        for out in outs:
            out[section * high : (section + 1) * high, :] = dense
    for away, out in enumerate(outs):
        start = pl.multiple_of((column ^ away) * rows, rows)
        out[panel_ref.shape[0] * high :, :] = tile_ref[pl.ds(start, rows), :]


def line_kernel(*refs):
    *parts, line, inverse = refs
    depth = line.shape[0] // len(parts)
    for away, part in enumerate(parts):
        line[away * depth : (away + 1) * depth, :] = part[:depth, :]
        inverse[:, away * LANES : (away + 1) * LANES] = part[depth:, :]


def pick_kernel(fold, blocks_here, listed_here, block_size, block_rows, inverse, out, turned):
    column = lax.axis_index("col")
    rows, order = inverse.shape
    cols = order // LANES
    turned[...] = inverse[...].T
    for section in range(out.shape[0]):
        pieces = []
        for away in range(cols):
            for block in range(listed_here):
                row = block_rows[section, (column ^ away) * listed_here + block]
                tile = (row // blocks_here) ^ column
                start = tile * LANES + (row % blocks_here) * block_size
                pieces.append(turned[pl.ds(pl.multiple_of(start, block_size), block_size), :])
        picked = jnp.concatenate(pieces, axis=0).T
        width = listed_here * block_size
        blank = jnp.zeros((rows, width), jnp.float32)
        folded = [
            jnp.concatenate(
                [
                    picked[:, away * width : (away + 1) * width] if i == j else blank
                    for away in range(cols)
                    for j in range(fold)
                ],
                axis=1,
            )
            for i in range(fold)
        ]
        high, low = split(jnp.concatenate(folded, axis=0))
        out[section] = jnp.concatenate([high, low], axis=0)


def couplings_kernel(couplings, high_ref, low_ref):
    high, low = split(couplings[...])
    high_ref[...] = high
    low_ref[...] = low


def product(stacked, high, low, dims):
    half = stacked.shape[0] // 2
    first = lax.dot_general(stacked, high, (dims, ((), ())), preferred_element_type=jnp.float32)
    second = lax.dot_general(stacked, low, (dims, ((), ())), preferred_element_type=jnp.float32)
    total = first + second
    return total[:half] + total[half:]


def finish_kernel(fold, count, cols, *refs):
    lines = refs[:count]
    picked, high_ref, low_ref, out = refs[count:]
    sections = out.shape[0]
    rows = out.shape[1]
    mine = lax.axis_index("row")
    depth = lines[0].shape[0] // cols // sections
    previous = None
    for section in range(sections):
        panel = jnp.concatenate(
            [
                jnp.concatenate(
                    [
                        line[(away * sections + section) * depth : (away * sections + section + 1) * depth, :]
                        for away in range(cols)
                    ],
                    axis=1,
                )
                for line in lines
            ],
            axis=0,
        )
        folded = product(picked[section], *split(panel), ((1,), (1,)))
        value = jnp.concatenate(
            [
                folded[i * rows : (i + 1) * rows, line * depth : (line + 1) * depth]
                for line in range(count)
                for i in range(fold)
            ],
            axis=1,
        )
        width = fold * depth
        step = 1
        while step < count:
            swapped = jnp.concatenate(
                [
                    value[:, (line ^ step) * width : ((line ^ step) + 1) * width]
                    for line in range(count)
                ],
                axis=1,
            )
            value = jnp.where((mine & step) != 0, swapped, value)
            step *= 2
        if previous is not None:
            stacked = jnp.concatenate(split(previous), axis=0)
            value = value + product(stacked, high_ref[section - 1], low_ref[section - 1], ((1,), (0,)))
        previous = -value
        out[section] = previous


def gathered(inverse_tiles, factor_panels, block_rows, couplings):
    f32 = jnp.float32
    sections, piece_rows, width = factor_panels.shape
    count, cols = lax.axis_size("row"), lax.axis_size("col")
    listed = block_rows.shape[1]
    block_size = width * cols // listed
    fold = LANES // width
    rows = inverse_tiles.shape[0] // cols
    order = inverse_tiles.shape[1] * cols
    depth = sections * piece_rows // fold

    packed = call(
        functools.partial(pack_kernel, rows, fold),
        [jax.ShapeDtypeStruct((depth + rows, LANES), f32)] * cols,
        [VMEM, VMEM],
        "pack",
    )(inverse_tiles, factor_panels)
    arrived = [packed[0]] + [swap(packed[away], "col", away) for away in range(1, cols)]
    line, inverse = call(
        line_kernel,
        [jax.ShapeDtypeStruct((cols * depth, LANES), f32), jax.ShapeDtypeStruct((rows, order), f32)],
        [VMEM] * cols,
        "line",
    )(*arrived)
    picked = call(
        functools.partial(pick_kernel, fold, LANES // block_size, listed // cols, block_size),
        jax.ShapeDtypeStruct((sections, 2 * fold * rows, cols * LANES), jnp.bfloat16),
        [SMEM, VMEM],
        "pick",
        [pltpu.VMEM((order, rows), f32)],
    )(block_rows, inverse)
    high, low = call(
        couplings_kernel,
        [jax.ShapeDtypeStruct(couplings.shape, jnp.bfloat16)] * 2,
        [VMEM],
        "couplings",
    )(couplings)
    lines = [line] + [None] * (count - 1)
    for chip in range(CORES, count, CORES):
        lines[chip] = swap(line, "row", chip)
    for chip in range(0, count, CORES):
        lines[chip + 1] = swap(lines[chip], "row", 1)
    return call(
        functools.partial(finish_kernel, fold, count, cols),
        jax.ShapeDtypeStruct((sections, rows, piece_rows * count), f32),
        [VMEM] * (count + 3),
        "finish",
    )(*lines, picked, high, low)


def on_device(inverse_tiles, factor_panels, block_rows, couplings):
    sections, piece_rows, width = factor_panels.shape
    count, cols = lax.axis_size("row"), lax.axis_size("col")
    powers = all(n & (n - 1) == 0 for n in (count, cols))
    fits = sections * piece_rows * width * count * cols * 4 <= REPLICA_BYTES
    lanes = inverse_tiles.shape[1] == LANES and LANES % width == 0
    body = gathered if powers and fits and lanes and count % CORES == 0 else streamed
    return body(inverse_tiles, factor_panels, block_rows, couplings)


def solution(mesh):
    return jax.shard_map(
        on_device,
        mesh=mesh,
        in_specs=(P("row", "col"), P(None, "row", "col"), P(), P()),
        out_specs=P(None, ("row", "col"), None),
        check_vma=False,
    )
```

```python
import functools

import jax
import jax.numpy as jnp
from jax import lax
from jax.experimental import pallas as pl
from jax.experimental.pallas import tpu as pltpu
from jax.sharding import PartitionSpec as P


LANES = 128
CORES = 2
REPLICA_BYTES = 4 << 20
KERNEL_BYTES = 12 << 20
VMEM = pl.BlockSpec(memory_space=pltpu.VMEM)
HBM = pl.BlockSpec(memory_space=pltpu.HBM)
SMEM = pl.BlockSpec(memory_space=pltpu.SMEM)


def streamed(inverse_tiles, factor_panels, block_rows, couplings):
    _, tile_cols = inverse_tiles.shape
    piece_rows = factor_panels.shape[1]
    listed = block_rows.shape[1]
    col_count = lax.axis_size("col")
    block_size = factor_panels.shape[2] * col_count // listed
    local_blocks = tile_cols // block_size
    my_column = lax.axis_index("col")
    offset = my_column * local_blocks
    targets = offset + jnp.arange(local_blocks, dtype=jnp.int32)
    results = []
    previous = None
    for section in range(factor_panels.shape[0]):
        section_rows = block_rows[section]
        gathered = lax.all_gather(factor_panels[section], "col", axis=1, tiled=True)
        onehot = (section_rows[:, None] == targets[None, :]).astype(jnp.float32)
        picked = jnp.einsum(
            "wpr,pq->wqr",
            gathered.reshape(piece_rows, listed, block_size),
            onehot,
            precision=lax.Precision.HIGHEST,
        ).reshape(piece_rows, tile_cols)
        partial_value = lax.dot_general(
            inverse_tiles,
            lax.all_gather(picked, "row", axis=0, tiled=True),
            (((1,), (1,)), ((), ())),
            precision=lax.Precision.HIGHEST,
            preferred_element_type=jnp.float32,
        )
        summed = lax.psum_scatter(partial_value, "col", scatter_dimension=0, tiled=True)
        if previous is not None:
            summed = summed + jnp.dot(
                previous,
                couplings[section - 1],
                precision=lax.Precision.HIGHEST,
                preferred_element_type=jnp.float32,
            )
        previous = -summed
        results.append(previous)
    return jnp.stack(results)


def call(kernel, out_shape, specs, scratch=()):
    run = pl.pallas_call(
        kernel,
        out_shape=out_shape,
        in_specs=specs,
        out_specs=jax.tree.map(lambda _: VMEM, out_shape),
        scratch_shapes=scratch,
        compiler_params=pltpu.CompilerParams(vmem_limit_bytes=KERNEL_BYTES),
    )
    return run


def split(value):
    high = value.astype(jnp.bfloat16)
    return high, (value - high.astype(jnp.float32)).astype(jnp.bfloat16)


def swap(value, axis, distance):
    count = lax.axis_size(axis)
    return lax.ppermute(value, axis, [(i, i ^ distance) for i in range(count)])


def pack_kernel(fold, panel_hbm, out, panel, arrived):
    copy = pltpu.make_async_copy(panel_hbm, panel, arrived)
    copy.start()
    copy.wait()
    high = panel.shape[1] // fold
    for section in range(panel.shape[0]):
        out[section * high : (section + 1) * high, :] = jnp.concatenate(
            [panel[section, i * high : (i + 1) * high, :] for i in range(fold)], axis=1
        )


def prepare_kernel(rows, tile_hbm, couplings_hbm, high_ref, low_ref, *rest):
    *shares, tile, couplings, tile_arrived, couplings_arrived = rest
    column = lax.axis_index("col")
    tile_copy = pltpu.make_async_copy(tile_hbm, tile, tile_arrived)
    couplings_copy = pltpu.make_async_copy(couplings_hbm, couplings, couplings_arrived)
    tile_copy.start()
    couplings_copy.start()
    tile_copy.wait()
    for away, share in enumerate(shares):
        start = pl.multiple_of((column ^ away) * rows, rows)
        share[...] = tile[pl.ds(start, rows), :]
    couplings_copy.wait()
    high, low = split(couplings[...])
    high_ref[...] = high
    low_ref[...] = low


def line_kernel(*refs):
    *parts, line = refs
    depth = line.shape[0] // len(parts)
    for away, part in enumerate(parts):
        line[away * depth : (away + 1) * depth, :] = part[...]


def pick_kernel(fold, blocks_here, listed_here, block_size, block_rows, *refs):
    *shares, out, turned = refs
    column = lax.axis_index("col")
    rows = shares[0].shape[0]
    cols = len(shares)
    turned[...] = jnp.concatenate([share[...] for share in shares], axis=1).T
    for section in range(out.shape[0]):
        pieces = []
        for away in range(cols):
            for block in range(listed_here):
                row = block_rows[section, (column ^ away) * listed_here + block]
                tile = (row // blocks_here) ^ column
                start = tile * LANES + (row % blocks_here) * block_size
                pieces.append(turned[pl.ds(pl.multiple_of(start, block_size), block_size), :])
        picked = jnp.concatenate(pieces, axis=0).T
        width = listed_here * block_size
        blank = jnp.zeros((rows, width), jnp.float32)
        folded = [
            jnp.concatenate(
                [
                    picked[:, away * width : (away + 1) * width] if i == j else blank
                    for away in range(cols)
                    for j in range(fold)
                ],
                axis=1,
            )
            for i in range(fold)
        ]
        high, low = split(jnp.concatenate(folded, axis=0))
        out[section] = jnp.concatenate([high, low], axis=0)


def product(stacked, high, low, dims):
    half = stacked.shape[0] // 2
    first = lax.dot_general(stacked, high, (dims, ((), ())), preferred_element_type=jnp.float32)
    second = lax.dot_general(stacked, low, (dims, ((), ())), preferred_element_type=jnp.float32)
    total = first + second
    return total[:half] + total[half:]


def finish_kernel(fold, count, cols, *refs):
    lines = refs[:count]
    picked, high_ref, low_ref, out = refs[count:]
    sections = out.shape[0]
    rows = out.shape[1]
    mine = lax.axis_index("row")
    depth = lines[0].shape[0] // cols // sections
    previous = None
    for section in range(sections):
        panel = jnp.concatenate(
            [
                jnp.concatenate(
                    [
                        line[(away * sections + section) * depth : (away * sections + section + 1) * depth, :]
                        for away in range(cols)
                    ],
                    axis=1,
                )
                for line in lines
            ],
            axis=0,
        )
        folded = product(picked[section], *split(panel), ((1,), (1,)))
        value = jnp.concatenate(
            [
                folded[i * rows : (i + 1) * rows, line * depth : (line + 1) * depth]
                for line in range(count)
                for i in range(fold)
            ],
            axis=1,
        )
        width = fold * depth
        step = 1
        while step < count:
            swapped = jnp.concatenate(
                [
                    value[:, (line ^ step) * width : ((line ^ step) + 1) * width]
                    for line in range(count)
                ],
                axis=1,
            )
            value = jnp.where((mine & step) != 0, swapped, value)
            step *= 2
        if previous is not None:
            stacked = jnp.concatenate(split(previous), axis=0)
            value = value + product(stacked, high_ref[section - 1], low_ref[section - 1], ((1,), (0,)))
        previous = -value
        out[section] = previous


def gathered(inverse_tiles, factor_panels, block_rows, couplings):
    f32 = jnp.float32
    sections, piece_rows, width = factor_panels.shape
    count, cols = lax.axis_size("row"), lax.axis_size("col")
    listed = block_rows.shape[1]
    block_size = width * cols // listed
    fold = LANES // width
    rows = inverse_tiles.shape[0] // cols
    order = inverse_tiles.shape[1] * cols
    depth = sections * piece_rows // fold

    own = call(
        functools.partial(pack_kernel, fold),
        jax.ShapeDtypeStruct((depth, LANES), f32),
        [HBM],
        [pltpu.VMEM(factor_panels.shape, f32), pltpu.SemaphoreType.DMA],
    )(factor_panels)
    parts = [own] + [swap(own, "col", away) for away in range(1, cols)]
    high, low, *shares = call(
        functools.partial(prepare_kernel, rows),
        [jax.ShapeDtypeStruct(couplings.shape, jnp.bfloat16)] * 2
        + [jax.ShapeDtypeStruct((rows, LANES), f32)] * cols,
        [HBM, HBM],
        [
            pltpu.VMEM(inverse_tiles.shape, f32),
            pltpu.VMEM(couplings.shape, f32),
            pltpu.SemaphoreType.DMA,
            pltpu.SemaphoreType.DMA,
        ],
    )(inverse_tiles, couplings)
    line = call(line_kernel, jax.ShapeDtypeStruct((cols * depth, LANES), f32), [VMEM] * cols)(*parts)
    lines = [line] + [None] * (count - 1)
    for chip in range(CORES, count, CORES):
        lines[chip] = swap(line, "row", chip)
    shares = shares[:1] + [swap(shares[away], "col", away) for away in range(1, cols)]
    picked = call(
        functools.partial(pick_kernel, fold, LANES // block_size, listed // cols, block_size),
        jax.ShapeDtypeStruct((sections, 2 * fold * rows, cols * LANES), jnp.bfloat16),
        [SMEM] + [VMEM] * cols,
        [pltpu.VMEM((order, rows), f32)],
    )(block_rows, *shares)
    for chip in range(0, count, CORES):
        lines[chip + 1] = swap(lines[chip], "row", 1)
    return call(
        functools.partial(finish_kernel, fold, count, cols),
        jax.ShapeDtypeStruct((sections, rows, piece_rows * count), f32),
        [VMEM] * (count + 3),
    )(*lines, picked, high, low)


def on_device(inverse_tiles, factor_panels, block_rows, couplings):
    sections, piece_rows, width = factor_panels.shape
    count, cols = lax.axis_size("row"), lax.axis_size("col")
    powers = all(n & (n - 1) == 0 for n in (count, cols))
    fits = sections * piece_rows * width * count * cols * 4 <= REPLICA_BYTES
    lanes = inverse_tiles.shape[1] == LANES and LANES % width == 0
    if powers and fits and lanes and count % CORES == 0:
        return gathered(inverse_tiles, factor_panels, block_rows, couplings)
    return streamed(inverse_tiles, factor_panels, block_rows, couplings)


def solution(mesh):
    return jax.shard_map(
        on_device,
        mesh=mesh,
        in_specs=(P("row", "col"), P(None, "row", "col"), P(), P()),
        out_specs=P(None, ("row", "col"), None),
        check_vma=False,
    )
```

```python
import functools

import jax
import jax.numpy as jnp
from jax import lax
from jax.experimental import pallas as pl
from jax.experimental.pallas import tpu as pltpu
from jax.sharding import PartitionSpec as P


LANES = 128
CORES = 2
REPLICA_BYTES = 4 << 20
KERNEL_BYTES = 12 << 20
VMEM = pl.BlockSpec(memory_space=pltpu.VMEM)
SMEM = pl.BlockSpec(memory_space=pltpu.SMEM)


def streamed(inverse_tiles, factor_panels, block_rows, couplings):
    _, tile_cols = inverse_tiles.shape
    piece_rows = factor_panels.shape[1]
    listed = block_rows.shape[1]
    col_count = lax.axis_size("col")
    block_size = factor_panels.shape[2] * col_count // listed
    local_blocks = tile_cols // block_size
    my_column = lax.axis_index("col")
    offset = my_column * local_blocks
    targets = offset + jnp.arange(local_blocks, dtype=jnp.int32)
    results = []
    previous = None
    for section in range(factor_panels.shape[0]):
        section_rows = block_rows[section]
        gathered = lax.all_gather(factor_panels[section], "col", axis=1, tiled=True)
        onehot = (section_rows[:, None] == targets[None, :]).astype(jnp.float32)
        picked = jnp.einsum(
            "wpr,pq->wqr",
            gathered.reshape(piece_rows, listed, block_size),
            onehot,
            precision=lax.Precision.HIGHEST,
        ).reshape(piece_rows, tile_cols)
        partial_value = lax.dot_general(
            inverse_tiles,
            lax.all_gather(picked, "row", axis=0, tiled=True),
            (((1,), (1,)), ((), ())),
            precision=lax.Precision.HIGHEST,
            preferred_element_type=jnp.float32,
        )
        summed = lax.psum_scatter(partial_value, "col", scatter_dimension=0, tiled=True)
        if previous is not None:
            summed = summed + jnp.dot(
                previous,
                couplings[section - 1],
                precision=lax.Precision.HIGHEST,
                preferred_element_type=jnp.float32,
            )
        previous = -summed
        results.append(previous)
    return jnp.stack(results)


def call(kernel, out_shape, specs, scratch=()):
    run = pl.pallas_call(
        kernel,
        out_shape=out_shape,
        in_specs=specs,
        out_specs=jax.tree.map(lambda _: VMEM, out_shape),
        scratch_shapes=scratch,
        compiler_params=pltpu.CompilerParams(vmem_limit_bytes=KERNEL_BYTES),
    )
    return run


def split(value):
    high = value.astype(jnp.bfloat16)
    return high, (value - high.astype(jnp.float32)).astype(jnp.bfloat16)


def swap(value, axis, distance):
    count = lax.axis_size(axis)
    return lax.ppermute(value, axis, [(i, i ^ distance) for i in range(count)])


def pack_kernel(rows, fold, tile_ref, panel_ref, *outs):
    column = lax.axis_index("col")
    high = panel_ref.shape[1] // fold
    for section in range(panel_ref.shape[0]):
        dense = jnp.concatenate(
            [panel_ref[section, i * high : (i + 1) * high, :] for i in range(fold)], axis=1
        )
        for out in outs:
            out[section * high : (section + 1) * high, :] = dense
    for away, out in enumerate(outs):
        start = pl.multiple_of((column ^ away) * rows, rows)
        out[panel_ref.shape[0] * high :, :] = tile_ref[pl.ds(start, rows), :]


def join_kernel(*refs):
    *parts, inverse, line = refs
    depth = line.shape[0] // len(parts)
    for away, part in enumerate(parts):
        inverse[:, away * LANES : (away + 1) * LANES] = part[depth:, :]
        line[away * depth : (away + 1) * depth, :] = part[:depth, :]


def couplings_kernel(couplings, high_ref, low_ref):
    high, low = split(couplings[...])
    high_ref[...] = high
    low_ref[...] = low


def place_kernel(fold, blocks_here, listed_here, block_size, block_rows, own_ref, other_ref, high_ref, low_ref):
    column = lax.axis_index("col")
    core = lax.rem(lax.axis_index("row"), CORES)
    sections = block_rows.shape[0]
    cols = high_ref.shape[0] // LANES
    width = listed_here * block_size
    depth = own_ref.shape[0] // cols // sections
    high_ref[...] = jnp.zeros_like(high_ref)
    low_ref[...] = jnp.zeros_like(low_ref)
    for section in range(sections):
        for first in range(0, cols, fold):
            pieces = []
            for e in range(CORES):
                parts = []
                for away in range(first, first + fold):
                    at = (away * sections + section) * depth
                    own, other = own_ref[at : at + depth, :], other_ref[at : at + depth, :]
                    parts.append(jnp.where(core == e, own, other))
                for i in range(fold):
                    pieces.append(
                        jnp.concatenate([part[:, i * width : (i + 1) * width] for part in parts], axis=1)
                    )
            high, low = split(jnp.concatenate(pieces, axis=0).T)
            for place in range(fold):
                for block in range(listed_here):
                    row = block_rows[section, (column ^ (first + place)) * listed_here + block]
                    tile = (row // blocks_here) ^ column
                    start = tile * LANES + (row % blocks_here) * block_size
                    target = pl.ds(pl.multiple_of(start, block_size), block_size)
                    at = place * width + block * block_size
                    lanes = slice(section * LANES, (section + 1) * LANES)
                    high_ref[target, lanes] = high[at : at + block_size]
                    low_ref[target, lanes] = low[at : at + block_size]


def product(stacked, high, low):
    half = stacked.shape[0] // 2
    first = jnp.dot(stacked, high, preferred_element_type=jnp.float32)
    second = jnp.dot(stacked, low, preferred_element_type=jnp.float32)
    total = first + second
    return total[:half] + total[half:]


def multiply_kernel(*refs):
    half = (len(refs) - 2) // 2
    inverses, (high_ref, low_ref), outs = refs[:half], refs[half : half + 2], refs[half + 2 :]
    rows = inverses[0].shape[0]
    stacked = jnp.concatenate(split(jnp.concatenate([ref[...] for ref in inverses], axis=0)), axis=0)
    total = product(stacked, high_ref[...], low_ref[...])
    for chip, out in enumerate(outs):
        for section in range(total.shape[1] // LANES):
            out[section * rows : (section + 1) * rows, :] = total[
                chip * rows : (chip + 1) * rows, section * LANES : (section + 1) * LANES
            ]


def finish_kernel(*refs):
    *parts, high_ref, low_ref, out = refs
    sections, rows, _ = out.shape
    chip = lax.div(lax.axis_index("row"), CORES)
    previous = None
    for section in range(sections):
        tiles = [part[section * rows : (section + 1) * rows, :] for part in parts]
        step = 1
        while step < len(tiles):
            tiles = [
                jnp.where((chip & step) != 0, tiles[i ^ step], tile) for i, tile in enumerate(tiles)
            ]
            step *= 2
        value = jnp.concatenate(tiles, axis=1)
        if previous is not None:
            stacked = jnp.concatenate(split(previous), axis=0)
            value = value + product(stacked, high_ref[section - 1], low_ref[section - 1])
        previous = -value
        out[section] = previous


def gathered(inverse_tiles, factor_panels, block_rows, couplings):
    f32 = jnp.float32
    sections, piece_rows, width = factor_panels.shape
    count, cols = lax.axis_size("row"), lax.axis_size("col")
    listed = block_rows.shape[1]
    block_size = width * cols // listed
    fold = LANES // width
    rows = inverse_tiles.shape[0] // cols
    order = inverse_tiles.shape[1] * cols
    depth = sections * piece_rows // fold

    bf16 = jnp.bfloat16
    chips = range(0, count, CORES)

    packed = call(
        functools.partial(pack_kernel, rows, fold),
        [jax.ShapeDtypeStruct((depth + rows, LANES), f32)] * cols,
        [VMEM, VMEM],
    )(inverse_tiles, factor_panels)
    arrived = [packed[0]] + [swap(packed[away], "col", away) for away in range(1, cols)]
    inverse, line = call(
        join_kernel,
        [jax.ShapeDtypeStruct((rows, order), f32), jax.ShapeDtypeStruct((cols * depth, LANES), f32)],
        [VMEM] * cols,
    )(*arrived)
    inverses = [inverse] + [swap(inverse, "row", chip) for chip in chips[1:]]
    placed = call(
        functools.partial(place_kernel, fold, LANES // block_size, listed // cols, block_size),
        [jax.ShapeDtypeStruct((order, sections * LANES), bf16)] * 2,
        [SMEM, VMEM, VMEM],
    )(block_rows, line, swap(line, "row", 1))
    products = call(
        multiply_kernel, [jax.ShapeDtypeStruct((sections * rows, LANES), f32)] * len(chips), [VMEM] * (len(chips) + 2)
    )(*inverses, *placed)
    returned = [products[0]] + [swap(products[i], "row", chip) for i, chip in enumerate(chips) if chip]
    halves = call(couplings_kernel, [jax.ShapeDtypeStruct(couplings.shape, bf16)] * 2, [VMEM])(couplings)
    return call(
        finish_kernel, jax.ShapeDtypeStruct((sections, rows, piece_rows * count), f32), [VMEM] * (len(chips) + 2)
    )(*returned, *halves)


def on_device(inverse_tiles, factor_panels, block_rows, couplings):
    sections, piece_rows, width = factor_panels.shape
    count, cols = lax.axis_size("row"), lax.axis_size("col")
    powers = all(n & (n - 1) == 0 for n in (count, cols))
    fits = sections * piece_rows * width * count * cols * 4 <= REPLICA_BYTES
    lanes = inverse_tiles.shape[1] == LANES == CORES * piece_rows and LANES % width == 0
    if powers and fits and lanes and count % CORES == 0 == cols % (LANES // width):
        return gathered(inverse_tiles, factor_panels, block_rows, couplings)
    return streamed(inverse_tiles, factor_panels, block_rows, couplings)


def solution(mesh):
    return jax.shard_map(
        on_device,
        mesh=mesh,
        in_specs=(P("row", "col"), P(None, "row", "col"), P(), P()),
        out_specs=P(None, ("row", "col"), None),
        check_vma=False,
    )
```

```python
import functools

import jax
import jax.numpy as jnp
from jax import lax
from jax.experimental import pallas as pl
from jax.experimental.pallas import tpu as pltpu
from jax.sharding import PartitionSpec as P


LANES = 128
CORES = 2
REPLICA_BYTES = 4 << 20
KERNEL_BYTES = 12 << 20
ANY = pl.BlockSpec(memory_space=pl.ANY)
VMEM = pl.BlockSpec(memory_space=pltpu.VMEM)
SMEM = pl.BlockSpec(memory_space=pltpu.SMEM)


def streamed(inverse_tiles, factor_panels, block_rows, couplings):
    _, tile_cols = inverse_tiles.shape
    piece_rows = factor_panels.shape[1]
    listed = block_rows.shape[1]
    col_count = lax.axis_size("col")
    block_size = factor_panels.shape[2] * col_count // listed
    local_blocks = tile_cols // block_size
    my_column = lax.axis_index("col")
    offset = my_column * local_blocks
    targets = offset + jnp.arange(local_blocks, dtype=jnp.int32)
    results = []
    previous = None
    for section in range(factor_panels.shape[0]):
        section_rows = block_rows[section]
        gathered = lax.all_gather(factor_panels[section], "col", axis=1, tiled=True)
        onehot = (section_rows[:, None] == targets[None, :]).astype(jnp.float32)
        picked = jnp.einsum(
            "wpr,pq->wqr",
            gathered.reshape(piece_rows, listed, block_size),
            onehot,
            precision=lax.Precision.HIGHEST,
        ).reshape(piece_rows, tile_cols)
        partial_value = lax.dot_general(
            inverse_tiles,
            lax.all_gather(picked, "row", axis=0, tiled=True),
            (((1,), (1,)), ((), ())),
            precision=lax.Precision.HIGHEST,
            preferred_element_type=jnp.float32,
        )
        summed = lax.psum_scatter(partial_value, "col", scatter_dimension=0, tiled=True)
        if previous is not None:
            summed = summed + jnp.dot(
                previous,
                couplings[section - 1],
                precision=lax.Precision.HIGHEST,
                preferred_element_type=jnp.float32,
            )
        previous = -summed
        results.append(previous)
    return jnp.stack(results)


def call(kernel, out_shape, specs, scratch=()):
    run = pl.pallas_call(
        kernel,
        out_shape=out_shape,
        in_specs=specs,
        out_specs=jax.tree.map(lambda _: VMEM, out_shape),
        scratch_shapes=scratch,
        compiler_params=pltpu.CompilerParams(vmem_limit_bytes=KERNEL_BYTES),
    )
    return run


def split(value):
    high = value.astype(jnp.bfloat16)
    return high, (value - high.astype(jnp.float32)).astype(jnp.bfloat16)


def swap(value, axis, distance):
    count = lax.axis_size(axis)
    return lax.ppermute(value, axis, [(i, i ^ distance) for i in range(count)])


def pack_kernel(rows, fold, tile_hbm, panel_hbm, *refs):
    *outs, tile, panel, tile_done, panel_done = refs
    column = lax.axis_index("col")
    tile_copy = pltpu.make_async_copy(tile_hbm, tile, tile_done)
    panel_copy = pltpu.make_async_copy(panel_hbm, panel, panel_done)
    panel_copy.start()
    tile_copy.start()
    high = panel.shape[1] // fold
    tile_copy.wait()
    for away, out in enumerate(outs):
        start = pl.multiple_of((column ^ away) * rows, rows)
        out[panel.shape[0] * high :, :] = tile[pl.ds(start, rows), :]
    panel_copy.wait()
    for section in range(panel.shape[0]):
        dense = jnp.concatenate(
            [panel[section, i * high : (i + 1) * high, :] for i in range(fold)], axis=1
        )
        for out in outs:
            out[section * high : (section + 1) * high, :] = dense


def join_kernel(*refs):
    *parts, inverse, line = refs
    depth = line.shape[0] // len(parts)
    for away, part in enumerate(parts):
        inverse[:, away * LANES : (away + 1) * LANES] = part[depth:, :]
        line[away * depth : (away + 1) * depth, :] = part[:depth, :]


def couplings_kernel(couplings, high_ref, low_ref):
    high, low = split(couplings[...])
    high_ref[...] = high
    low_ref[...] = low


def place_kernel(fold, blocks_here, listed_here, block_size, block_rows, own_ref, other_ref, high_ref, low_ref):
    column = lax.axis_index("col")
    core = lax.rem(lax.axis_index("row"), CORES)
    sections = block_rows.shape[0]
    cols = high_ref.shape[0] // LANES
    width = listed_here * block_size
    depth = own_ref.shape[0] // cols // sections
    high_ref[...] = jnp.zeros_like(high_ref)
    low_ref[...] = jnp.zeros_like(low_ref)
    for section in range(sections):
        for first in range(0, cols, fold):
            pieces = []
            for e in range(CORES):
                parts = []
                for away in range(first, first + fold):
                    at = (away * sections + section) * depth
                    own, other = own_ref[at : at + depth, :], other_ref[at : at + depth, :]
                    parts.append(jnp.where(core == e, own, other))
                for i in range(fold):
                    pieces.append(
                        jnp.concatenate([part[:, i * width : (i + 1) * width] for part in parts], axis=1)
                    )
            high, low = split(jnp.concatenate(pieces, axis=0).T)
            for place in range(fold):
                for block in range(listed_here):
                    row = block_rows[section, (column ^ (first + place)) * listed_here + block]
                    tile = (row // blocks_here) ^ column
                    start = tile * LANES + (row % blocks_here) * block_size
                    target = pl.ds(pl.multiple_of(start, block_size), block_size)
                    at = place * width + block * block_size
                    lanes = slice(section * LANES, (section + 1) * LANES)
                    high_ref[target, lanes] = high[at : at + block_size]
                    low_ref[target, lanes] = low[at : at + block_size]


def product(stacked, high, low):
    half = stacked.shape[0] // 2
    first = jnp.dot(stacked, high, preferred_element_type=jnp.float32)
    second = jnp.dot(stacked, low, preferred_element_type=jnp.float32)
    total = first + second
    return total[:half] + total[half:]


def multiply_kernel(*refs):
    half = (len(refs) - 2) // 2
    inverses, (high_ref, low_ref), outs = refs[:half], refs[half : half + 2], refs[half + 2 :]
    rows = inverses[0].shape[0]
    stacked = jnp.concatenate(split(jnp.concatenate([ref[...] for ref in inverses], axis=0)), axis=0)
    total = product(stacked, high_ref[...], low_ref[...])
    for chip, out in enumerate(outs):
        for section in range(total.shape[1] // LANES):
            out[section * rows : (section + 1) * rows, :] = total[
                chip * rows : (chip + 1) * rows, section * LANES : (section + 1) * LANES
            ]


def finish_kernel(*refs):
    *parts, high_ref, low_ref, out = refs
    sections, rows, _ = out.shape
    chip = lax.div(lax.axis_index("row"), CORES)
    previous = None
    for section in range(sections):
        tiles = [part[section * rows : (section + 1) * rows, :] for part in parts]
        step = 1
        while step < len(tiles):
            tiles = [
                jnp.where((chip & step) != 0, tiles[i ^ step], tile) for i, tile in enumerate(tiles)
            ]
            step *= 2
        value = jnp.concatenate(tiles, axis=1)
        if previous is not None:
            stacked = jnp.concatenate(split(previous), axis=0)
            value = value + product(stacked, high_ref[section - 1], low_ref[section - 1])
        previous = -value
        out[section] = previous


def gathered(inverse_tiles, factor_panels, block_rows, couplings):
    f32 = jnp.float32
    sections, piece_rows, width = factor_panels.shape
    count, cols = lax.axis_size("row"), lax.axis_size("col")
    listed = block_rows.shape[1]
    block_size = width * cols // listed
    fold = LANES // width
    rows = inverse_tiles.shape[0] // cols
    order = inverse_tiles.shape[1] * cols
    depth = sections * piece_rows // fold

    bf16 = jnp.bfloat16
    chips = range(0, count, CORES)

    packed = call(
        functools.partial(pack_kernel, rows, fold),
        [jax.ShapeDtypeStruct((depth + rows, LANES), f32)] * cols,
        [ANY, ANY],
        [
            pltpu.VMEM(inverse_tiles.shape, f32),
            pltpu.VMEM(factor_panels.shape, f32),
            pltpu.SemaphoreType.DMA,
            pltpu.SemaphoreType.DMA,
        ],
    )(*[pltpu.with_memory_space_constraint(x, pltpu.HBM) for x in (inverse_tiles, factor_panels)])
    arrived = [packed[0]] + [swap(packed[away], "col", away) for away in range(1, cols)]
    inverse, line = call(
        join_kernel,
        [jax.ShapeDtypeStruct((rows, order), f32), jax.ShapeDtypeStruct((cols * depth, LANES), f32)],
        [VMEM] * cols,
    )(*arrived)
    inverses = [inverse] + [swap(inverse, "row", chip) for chip in chips[1:]]
    placed = call(
        functools.partial(place_kernel, fold, LANES // block_size, listed // cols, block_size),
        [jax.ShapeDtypeStruct((order, sections * LANES), bf16)] * 2,
        [SMEM, VMEM, VMEM],
    )(block_rows, line, swap(line, "row", 1))
    products = call(
        multiply_kernel, [jax.ShapeDtypeStruct((sections * rows, LANES), f32)] * len(chips), [VMEM] * (len(chips) + 2)
    )(*inverses, *placed)
    returned = [products[0]] + [swap(products[i], "row", chip) for i, chip in enumerate(chips) if chip]
    halves = call(couplings_kernel, [jax.ShapeDtypeStruct(couplings.shape, bf16)] * 2, [VMEM])(couplings)
    return call(
        finish_kernel, jax.ShapeDtypeStruct((sections, rows, piece_rows * count), f32), [VMEM] * (len(chips) + 2)
    )(*returned, *halves)


def on_device(inverse_tiles, factor_panels, block_rows, couplings):
    sections, piece_rows, width = factor_panels.shape
    count, cols = lax.axis_size("row"), lax.axis_size("col")
    powers = all(n & (n - 1) == 0 for n in (count, cols))
    fits = sections * piece_rows * width * count * cols * 4 <= REPLICA_BYTES
    lanes = inverse_tiles.shape[1] == LANES == CORES * piece_rows and LANES % width == 0
    if powers and fits and lanes and count % CORES == 0 == cols % (LANES // width):
        return gathered(inverse_tiles, factor_panels, block_rows, couplings)
    return streamed(inverse_tiles, factor_panels, block_rows, couplings)


def solution(mesh):
    return jax.shard_map(
        on_device,
        mesh=mesh,
        in_specs=(P("row", "col"), P(None, "row", "col"), P(), P()),
        out_specs=P(None, ("row", "col"), None),
        check_vma=False,
    )
```

```python
import functools

import jax
import jax.numpy as jnp
from jax import lax
from jax.experimental import pallas as pl
from jax.experimental.pallas import tpu as pltpu
from jax.sharding import PartitionSpec as P


LANES = 128
CORES = 2
REPLICA_BYTES = 4 << 20
KERNEL_BYTES = 12 << 20
ANY = pl.BlockSpec(memory_space=pl.ANY)
VMEM = pl.BlockSpec(memory_space=pltpu.VMEM)
SMEM = pl.BlockSpec(memory_space=pltpu.SMEM)


def streamed(inverse_tiles, factor_panels, block_rows, couplings):
    _, tile_cols = inverse_tiles.shape
    piece_rows = factor_panels.shape[1]
    listed = block_rows.shape[1]
    col_count = lax.axis_size("col")
    block_size = factor_panels.shape[2] * col_count // listed
    local_blocks = tile_cols // block_size
    my_column = lax.axis_index("col")
    offset = my_column * local_blocks
    targets = offset + jnp.arange(local_blocks, dtype=jnp.int32)
    results = []
    previous = None
    for section in range(factor_panels.shape[0]):
        section_rows = block_rows[section]
        gathered = lax.all_gather(factor_panels[section], "col", axis=1, tiled=True)
        onehot = (section_rows[:, None] == targets[None, :]).astype(jnp.float32)
        picked = jnp.einsum(
            "wpr,pq->wqr",
            gathered.reshape(piece_rows, listed, block_size),
            onehot,
            precision=lax.Precision.HIGHEST,
        ).reshape(piece_rows, tile_cols)
        partial_value = lax.dot_general(
            inverse_tiles,
            lax.all_gather(picked, "row", axis=0, tiled=True),
            (((1,), (1,)), ((), ())),
            precision=lax.Precision.HIGHEST,
            preferred_element_type=jnp.float32,
        )
        summed = lax.psum_scatter(partial_value, "col", scatter_dimension=0, tiled=True)
        if previous is not None:
            summed = summed + jnp.dot(
                previous,
                couplings[section - 1],
                precision=lax.Precision.HIGHEST,
                preferred_element_type=jnp.float32,
            )
        previous = -summed
        results.append(previous)
    return jnp.stack(results)


def call(kernel, out_shape, specs, scratch=()):
    run = pl.pallas_call(
        kernel,
        out_shape=out_shape,
        in_specs=specs,
        out_specs=jax.tree.map(lambda _: VMEM, out_shape),
        scratch_shapes=scratch,
        compiler_params=pltpu.CompilerParams(vmem_limit_bytes=KERNEL_BYTES),
    )
    return run


def split(value):
    high = value.astype(jnp.bfloat16)
    return high, (value - high.astype(jnp.float32)).astype(jnp.bfloat16)


def swap(value, axis, distances):
    pairs = [(i, i ^ distances[i % len(distances)]) for i in range(lax.axis_size(axis))]
    return lax.ppermute(value, axis, pairs)


def pack_kernel(rows, fold, tile_hbm, panel_hbm, *refs):
    *outs, tile, panel, tile_done, panel_done = refs
    column = lax.axis_index("col")
    tile_copy = pltpu.make_async_copy(tile_hbm, tile, tile_done)
    panel_copy = pltpu.make_async_copy(panel_hbm, panel, panel_done)
    panel_copy.start()
    tile_copy.start()
    high = panel.shape[1] // fold
    tile_copy.wait()
    for away, out in enumerate(outs):
        start = pl.multiple_of((column ^ away) * rows, rows)
        out[panel.shape[0] * high :, :] = tile[pl.ds(start, rows), :]
    panel_copy.wait()
    for section in range(panel.shape[0]):
        dense = jnp.concatenate(
            [panel[section, i * high : (i + 1) * high, :] for i in range(fold)], axis=1
        )
        for out in outs:
            out[section * high : (section + 1) * high, :] = dense


def join_kernel(*refs):
    *parts, inverse, line = refs
    depth = line.shape[0] // len(parts)
    for away, part in enumerate(parts):
        inverse[:, away * LANES : (away + 1) * LANES] = part[depth:, :]
        line[away * depth : (away + 1) * depth, :] = part[:depth, :]


def both_kernel(own, other, out):
    rows = own.shape[0]
    core = lax.rem(lax.axis_index("row"), CORES)
    out[pl.ds(pl.multiple_of(core * rows, rows), rows), :] = own[...]
    out[pl.ds(pl.multiple_of((CORES - 1 - core) * rows, rows), rows), :] = other[...]


def couplings_kernel(couplings, high_ref, low_ref):
    high, low = split(couplings[...])
    high_ref[...] = high
    low_ref[...] = low


def place_kernel(fold, blocks_here, listed_here, block_size, block_rows, own_ref, other_ref, high_ref, low_ref):
    column = lax.axis_index("col")
    core = lax.rem(lax.axis_index("row"), CORES)
    sections = block_rows.shape[0]
    cols = high_ref.shape[0] // LANES
    width = listed_here * block_size
    depth = own_ref.shape[0] // cols // sections
    high_ref[...] = jnp.zeros_like(high_ref)
    low_ref[...] = jnp.zeros_like(low_ref)
    for section in range(sections):
        for first in range(0, cols, fold):
            pieces = []
            for e in range(CORES):
                parts = []
                for away in range(first, first + fold):
                    at = (away * sections + section) * depth
                    own, other = own_ref[at : at + depth, :], other_ref[at : at + depth, :]
                    parts.append(jnp.where(core == e, own, other))
                for i in range(fold):
                    pieces.append(
                        jnp.concatenate([part[:, i * width : (i + 1) * width] for part in parts], axis=1)
                    )
            high, low = split(jnp.concatenate(pieces, axis=0).T)
            for place in range(fold):
                for block in range(listed_here):
                    row = block_rows[section, (column ^ (first + place)) * listed_here + block]
                    tile = (row // blocks_here) ^ column
                    start = tile * LANES + (row % blocks_here) * block_size
                    target = pl.ds(pl.multiple_of(start, block_size), block_size)
                    at = place * width + block * block_size
                    lanes = slice(section * LANES, (section + 1) * LANES)
                    high_ref[target, lanes] = high[at : at + block_size]
                    low_ref[target, lanes] = low[at : at + block_size]


def product(stacked, high, low):
    half = stacked.shape[0] // 2
    first = jnp.dot(stacked, high, preferred_element_type=jnp.float32)
    second = jnp.dot(stacked, low, preferred_element_type=jnp.float32)
    total = first + second
    return total[:half] + total[half:]


def multiply_kernel(*refs):
    half = (len(refs) - 2) // 2
    inverses, (high_ref, low_ref), outs = refs[:half], refs[half : half + 2], refs[half + 2 :]
    rows = inverses[0].shape[0]
    stacked = jnp.concatenate(split(jnp.concatenate([ref[...] for ref in inverses], axis=0)), axis=0)
    total = product(stacked, high_ref[...], low_ref[...])
    sections = total.shape[1] // LANES
    start = 0
    for out in outs:
        for at in range(0, out.shape[0], rows):
            section = at // rows % sections
            out[at : at + rows, :] = total[start : start + rows, section * LANES : (section + 1) * LANES]
            if section == sections - 1:
                start += rows


def other_kernel(pair, out):
    size = out.shape[0]
    core = lax.rem(lax.axis_index("row"), CORES)
    out[...] = pair[pl.ds(pl.multiple_of((CORES - 1 - core) * size, size), size), :]


def finish_kernel(own, near, far, handed, high_ref, low_ref, out):
    sections, rows, _ = out.shape
    chip = lax.div(lax.axis_index("row"), CORES)
    core = lax.rem(lax.axis_index("row"), CORES)
    size = sections * rows
    previous = None
    for section in range(sections):
        at = section * rows
        kept = far[pl.ds(pl.multiple_of(core * size + at, rows), rows), :]
        given = handed[at : at + rows, :]
        tiles = [
            own[at : at + rows, :],
            jnp.where(core == 0, kept, given),
            near[at : at + rows, :],
            jnp.where(core == 0, given, kept),
        ]
        step = 1
        while step < len(tiles):
            tiles = [
                jnp.where((chip & step) != 0, tiles[i ^ step], tile) for i, tile in enumerate(tiles)
            ]
            step *= 2
        value = jnp.concatenate(tiles, axis=1)
        if previous is not None:
            stacked = jnp.concatenate(split(previous), axis=0)
            value = value + product(stacked, high_ref[section - 1], low_ref[section - 1])
        previous = -value
        out[section] = previous


def gathered(inverse_tiles, factor_panels, block_rows, couplings):
    f32 = jnp.float32
    sections, piece_rows, width = factor_panels.shape
    count, cols = lax.axis_size("row"), lax.axis_size("col")
    listed = block_rows.shape[1]
    block_size = width * cols // listed
    fold = LANES // width
    rows = inverse_tiles.shape[0] // cols
    order = inverse_tiles.shape[1] * cols
    depth = sections * piece_rows // fold

    bf16 = jnp.bfloat16
    beside, along, across = ([CORES * i] for i in (1, 2, 3))
    pair, far = [1], beside + across

    packed = call(
        functools.partial(pack_kernel, rows, fold),
        [jax.ShapeDtypeStruct((depth + rows, LANES), f32)] * cols,
        [ANY, ANY],
        [
            pltpu.VMEM(inverse_tiles.shape, f32),
            pltpu.VMEM(factor_panels.shape, f32),
            pltpu.SemaphoreType.DMA,
            pltpu.SemaphoreType.DMA,
        ],
    )(*[pltpu.with_memory_space_constraint(x, pltpu.HBM) for x in (inverse_tiles, factor_panels)])
    arrived = [packed[0]] + [swap(packed[away], "col", [away]) for away in range(1, cols)]
    inverse, line = call(
        join_kernel,
        [jax.ShapeDtypeStruct((rows, order), f32), jax.ShapeDtypeStruct((cols * depth, LANES), f32)],
        [VMEM] * cols,
    )(*arrived)
    other, other_line = swap(inverse, "row", pair), swap(line, "row", pair)
    both = call(both_kernel, jax.ShapeDtypeStruct((CORES * rows, order), f32), [VMEM, VMEM])(inverse, other)
    inverses = [inverse, swap(inverse, "row", along), swap(both, "row", far)]
    placed = call(
        functools.partial(place_kernel, fold, LANES // block_size, listed // cols, block_size),
        [jax.ShapeDtypeStruct((order, sections * LANES), bf16)] * 2,
        [SMEM, VMEM, VMEM],
    )(block_rows, line, other_line)
    own, to_near, to_far = call(
        multiply_kernel,
        [jax.ShapeDtypeStruct((n * sections * rows, LANES), f32) for n in (1, 1, CORES)],
        [VMEM] * (len(inverses) + 2),
    )(*inverses, *placed)
    from_far = swap(to_far, "row", far)
    from_near = swap(to_near, "row", along)
    handed = swap(
        call(other_kernel, jax.ShapeDtypeStruct((sections * rows, LANES), f32), [VMEM])(from_far), "row", pair
    )
    halves = call(couplings_kernel, [jax.ShapeDtypeStruct(couplings.shape, bf16)] * 2, [VMEM])(couplings)
    return call(
        finish_kernel, jax.ShapeDtypeStruct((sections, rows, piece_rows * count), f32), [VMEM] * 6
    )(own, from_near, from_far, handed, *halves)


def on_device(inverse_tiles, factor_panels, block_rows, couplings):
    sections, piece_rows, width = factor_panels.shape
    count, cols = lax.axis_size("row"), lax.axis_size("col")
    powers = all(n & (n - 1) == 0 for n in (count, cols))
    fits = sections * piece_rows * width * count * cols * 4 <= REPLICA_BYTES
    lanes = inverse_tiles.shape[1] == LANES == CORES * piece_rows and LANES % width == 0
    square = count == 4 * CORES
    if powers and fits and lanes and square and cols % (LANES // width) == 0:
        return gathered(inverse_tiles, factor_panels, block_rows, couplings)
    return streamed(inverse_tiles, factor_panels, block_rows, couplings)


def solution(mesh):
    return jax.shard_map(
        on_device,
        mesh=mesh,
        in_specs=(P("row", "col"), P(None, "row", "col"), P(), P()),
        out_specs=P(None, ("row", "col"), None),
        check_vma=False,
    )
```

```python
import functools

import jax
import jax.numpy as jnp
from jax import lax
from jax.experimental import pallas as pl
from jax.experimental.pallas import tpu as pltpu
from jax.sharding import PartitionSpec as P


LANES = 128
CORES = 2
REPLICA_BYTES = 4 << 20
KERNEL_BYTES = 12 << 20
ANY = pl.BlockSpec(memory_space=pl.ANY)
VMEM = pl.BlockSpec(memory_space=pltpu.VMEM)
SMEM = pl.BlockSpec(memory_space=pltpu.SMEM)


def streamed(inverse_tiles, factor_panels, block_rows, couplings):
    _, tile_cols = inverse_tiles.shape
    piece_rows = factor_panels.shape[1]
    listed = block_rows.shape[1]
    col_count = lax.axis_size("col")
    block_size = factor_panels.shape[2] * col_count // listed
    local_blocks = tile_cols // block_size
    my_column = lax.axis_index("col")
    offset = my_column * local_blocks
    targets = offset + jnp.arange(local_blocks, dtype=jnp.int32)
    results = []
    previous = None
    for section in range(factor_panels.shape[0]):
        section_rows = block_rows[section]
        gathered = lax.all_gather(factor_panels[section], "col", axis=1, tiled=True)
        onehot = (section_rows[:, None] == targets[None, :]).astype(jnp.float32)
        picked = jnp.einsum(
            "wpr,pq->wqr",
            gathered.reshape(piece_rows, listed, block_size),
            onehot,
            precision=lax.Precision.HIGHEST,
        ).reshape(piece_rows, tile_cols)
        partial_value = lax.dot_general(
            inverse_tiles,
            lax.all_gather(picked, "row", axis=0, tiled=True),
            (((1,), (1,)), ((), ())),
            precision=lax.Precision.HIGHEST,
            preferred_element_type=jnp.float32,
        )
        summed = lax.psum_scatter(partial_value, "col", scatter_dimension=0, tiled=True)
        if previous is not None:
            summed = summed + jnp.dot(
                previous,
                couplings[section - 1],
                precision=lax.Precision.HIGHEST,
                preferred_element_type=jnp.float32,
            )
        previous = -summed
        results.append(previous)
    return jnp.stack(results)


def call(kernel, out_shape, specs, scratch=()):
    run = pl.pallas_call(
        kernel,
        out_shape=out_shape,
        in_specs=specs,
        out_specs=jax.tree.map(lambda _: VMEM, out_shape),
        scratch_shapes=scratch,
        compiler_params=pltpu.CompilerParams(vmem_limit_bytes=KERNEL_BYTES),
    )
    return run


def split(value):
    high = value.astype(jnp.bfloat16)
    return high, (value - high.astype(jnp.float32)).astype(jnp.bfloat16)


def swap(value, axis, distances):
    pairs = [(i, i ^ distances[i % len(distances)]) for i in range(lax.axis_size(axis))]
    return lax.ppermute(value, axis, pairs)


def pack_kernel(rows, fold, tile_hbm, panel_hbm, *refs):
    *outs, tile, panel, tile_done, panel_done = refs
    column = lax.axis_index("col")
    tile_copy = pltpu.make_async_copy(tile_hbm, tile, tile_done)
    panel_copy = pltpu.make_async_copy(panel_hbm, panel, panel_done)
    panel_copy.start()
    tile_copy.start()
    high = panel.shape[1] // fold
    tile_copy.wait()
    for away, out in enumerate(outs):
        start = pl.multiple_of((column ^ away) * rows, rows)
        out[panel.shape[0] * high :, :] = tile[pl.ds(start, rows), :]
    panel_copy.wait()
    for section in range(panel.shape[0]):
        dense = jnp.concatenate(
            [panel[section, i * high : (i + 1) * high, :] for i in range(fold)], axis=1
        )
        for out in outs:
            out[section * high : (section + 1) * high, :] = dense


def join_kernel(*refs):
    *parts, inverse, line = refs
    depth = line.shape[0] // len(parts)
    for away, part in enumerate(parts):
        inverse[:, away * LANES : (away + 1) * LANES] = part[depth:, :]
        line[away * depth : (away + 1) * depth, :] = part[:depth, :]


def both_kernel(own, other, out):
    rows = own.shape[0]
    core = lax.rem(lax.axis_index("row"), CORES)
    out[pl.ds(pl.multiple_of(core * rows, rows), rows), :] = own[...]
    out[pl.ds(pl.multiple_of((CORES - 1 - core) * rows, rows), rows), :] = other[...]


def chains(sections):
    return [(first, last) for last in range(1, sections) for first in reversed(range(last))]


def couplings_kernel(couplings, high_ref, low_ref):
    order = chains(couplings.shape[0] + 1)
    for at, (first, last) in enumerate(order):
        if first == last - 1:
            value = couplings[first]
        else:
            stacked = jnp.concatenate(split(couplings[first]), axis=0)
            after = order.index((first + 1, last))
            value = product(stacked, high_ref[after], low_ref[after])
        high_ref[at], low_ref[at] = split(value)


def place_kernel(fold, blocks_here, listed_here, block_size, block_rows, own_ref, other_ref, high_ref, low_ref):
    column = lax.axis_index("col")
    core = lax.rem(lax.axis_index("row"), CORES)
    sections = block_rows.shape[0]
    cols = high_ref.shape[0] // LANES
    width = listed_here * block_size
    depth = own_ref.shape[0] // cols // sections
    high_ref[...] = jnp.zeros_like(high_ref)
    low_ref[...] = jnp.zeros_like(low_ref)
    for section in range(sections):
        for first in range(0, cols, fold):
            pieces = []
            for e in range(CORES):
                parts = []
                for away in range(first, first + fold):
                    at = (away * sections + section) * depth
                    own, other = own_ref[at : at + depth, :], other_ref[at : at + depth, :]
                    parts.append(jnp.where(core == e, own, other))
                for i in range(fold):
                    pieces.append(
                        jnp.concatenate([part[:, i * width : (i + 1) * width] for part in parts], axis=1)
                    )
            high, low = split(jnp.concatenate(pieces, axis=0).T)
            for place in range(fold):
                for block in range(listed_here):
                    row = block_rows[section, (column ^ (first + place)) * listed_here + block]
                    tile = (row // blocks_here) ^ column
                    start = tile * LANES + (row % blocks_here) * block_size
                    target = pl.ds(pl.multiple_of(start, block_size), block_size)
                    at = place * width + block * block_size
                    lanes = slice(section * LANES, (section + 1) * LANES)
                    high_ref[target, lanes] = high[at : at + block_size]
                    low_ref[target, lanes] = low[at : at + block_size]


def product(stacked, high, low):
    half = stacked.shape[0] // 2
    first = jnp.dot(stacked, high, preferred_element_type=jnp.float32)
    second = jnp.dot(stacked, low, preferred_element_type=jnp.float32)
    total = first + second
    return total[:half] + total[half:]


def multiply_kernel(*refs):
    half = (len(refs) - 2) // 2
    inverses, (high_ref, low_ref), outs = refs[:half], refs[half : half + 2], refs[half + 2 :]
    rows = inverses[0].shape[0]
    stacked = jnp.concatenate(split(jnp.concatenate([ref[...] for ref in inverses], axis=0)), axis=0)
    total = product(stacked, high_ref[...], low_ref[...])
    sections = total.shape[1] // LANES
    start = 0
    for out in outs:
        for at in range(0, out.shape[0], rows):
            section = at // rows % sections
            out[at : at + rows, :] = total[start : start + rows, section * LANES : (section + 1) * LANES]
            if section == sections - 1:
                start += rows


def other_kernel(pair, out):
    size = out.shape[0]
    core = lax.rem(lax.axis_index("row"), CORES)
    out[...] = pair[pl.ds(pl.multiple_of((CORES - 1 - core) * size, size), size), :]


def chained(values, high_ref, low_ref, blocks):
    def rows(ref, at):
        return jnp.concatenate([ref[at, block, :] for block in blocks], axis=0)

    order = chains(len(values))
    stacks = [jnp.concatenate(split(value), axis=0) for value in values]
    totals = []
    for last in range(len(values)):
        total = None
        for first in range(last):
            at = order.index((first, last))
            term = product(stacks[first], rows(high_ref, at), rows(low_ref, at))
            term = term if (last - first) % 2 else -term
            total = term if total is None else total + term
        totals.append(total)
    return totals


def blocks_of(*distances):
    chip = lax.div(lax.axis_index("row"), CORES)
    return [pl.ds(pl.multiple_of((chip ^ away) * LANES, LANES), LANES) for away in distances]


def advance(start, parts, blocks, high_ref, low_ref, out):
    sections, rows, _ = out.shape
    values = [
        [part[section * rows : (section + 1) * rows, :] for part in parts] for section in range(sections)
    ]
    totals = chained([jnp.concatenate(value, axis=1) for value in values], high_ref, low_ref, blocks)
    for section, total in enumerate(totals):
        base = jnp.zeros(out.shape[1:], jnp.float32) if start is None else start[section]
        out[section] = base if total is None else base + total
        for block, value in zip(blocks, values[section]):
            out[section, :, block] = out[section, :, block] - value


def partial_kernel(own, far, high_ref, low_ref, out):
    core = lax.rem(lax.axis_index("row"), CORES)
    size = own.shape[0]
    kept = far.at[pl.ds(pl.multiple_of(core * size, size), size), :]
    advance(None, [own, kept], blocks_of(0, jnp.where(core == 0, 1, 3)), high_ref, low_ref, out)


def finish_kernel(partial, near, handed, high_ref, low_ref, out):
    core = lax.rem(lax.axis_index("row"), CORES)
    advance(partial, [near, handed], blocks_of(2, jnp.where(core == 0, 3, 1)), high_ref, low_ref, out)


def gathered(inverse_tiles, factor_panels, block_rows, couplings):
    f32 = jnp.float32
    sections, piece_rows, width = factor_panels.shape
    count, cols = lax.axis_size("row"), lax.axis_size("col")
    listed = block_rows.shape[1]
    block_size = width * cols // listed
    fold = LANES // width
    rows = inverse_tiles.shape[0] // cols
    order = inverse_tiles.shape[1] * cols
    depth = sections * piece_rows // fold

    bf16 = jnp.bfloat16
    beside, along, across = ([CORES * i] for i in (1, 2, 3))
    pair, far = [1], beside + across

    packed = call(
        functools.partial(pack_kernel, rows, fold),
        [jax.ShapeDtypeStruct((depth + rows, LANES), f32)] * cols,
        [ANY, ANY],
        [
            pltpu.VMEM(inverse_tiles.shape, f32),
            pltpu.VMEM(factor_panels.shape, f32),
            pltpu.SemaphoreType.DMA,
            pltpu.SemaphoreType.DMA,
        ],
    )(*[pltpu.with_memory_space_constraint(x, pltpu.HBM) for x in (inverse_tiles, factor_panels)])
    arrived = [packed[0]] + [swap(packed[away], "col", [away]) for away in range(1, cols)]
    inverse, line = call(
        join_kernel,
        [jax.ShapeDtypeStruct((rows, order), f32), jax.ShapeDtypeStruct((cols * depth, LANES), f32)],
        [VMEM] * cols,
    )(*arrived)
    other, other_line = swap(inverse, "row", pair), swap(line, "row", pair)
    both = call(both_kernel, jax.ShapeDtypeStruct((CORES * rows, order), f32), [VMEM, VMEM])(inverse, other)
    inverses = [inverse, swap(inverse, "row", along), swap(both, "row", far)]
    placed = call(
        functools.partial(place_kernel, fold, LANES // block_size, listed // cols, block_size),
        [jax.ShapeDtypeStruct((order, sections * LANES), bf16)] * 2,
        [SMEM, VMEM, VMEM],
    )(block_rows, line, other_line)
    own, to_near, to_far = call(
        multiply_kernel,
        [jax.ShapeDtypeStruct((n * sections * rows, LANES), f32) for n in (1, 1, CORES)],
        [VMEM] * (len(inverses) + 2),
    )(*inverses, *placed)
    from_far = swap(to_far, "row", far)
    from_near = swap(to_near, "row", along)
    handed = swap(
        call(other_kernel, jax.ShapeDtypeStruct((sections * rows, LANES), f32), [VMEM])(from_far), "row", pair
    )
    halves = call(
        couplings_kernel, [jax.ShapeDtypeStruct((len(chains(sections)),) + couplings.shape[1:], bf16)] * 2, [VMEM]
    )(couplings)
    result = jax.ShapeDtypeStruct((sections, rows, piece_rows * count), f32)
    partial = call(partial_kernel, result, [VMEM] * 4)(own, from_far, *halves)
    return call(finish_kernel, result, [VMEM] * 5)(partial, from_near, handed, *halves)


def on_device(inverse_tiles, factor_panels, block_rows, couplings):
    sections, piece_rows, width = factor_panels.shape
    count, cols = lax.axis_size("row"), lax.axis_size("col")
    powers = all(n & (n - 1) == 0 for n in (count, cols))
    fits = sections * piece_rows * width * count * cols * 4 <= REPLICA_BYTES
    lanes = inverse_tiles.shape[1] == LANES == CORES * piece_rows and LANES % width == 0
    square = count == 4 * CORES
    if powers and fits and lanes and square and cols % (LANES // width) == 0:
        return gathered(inverse_tiles, factor_panels, block_rows, couplings)
    return streamed(inverse_tiles, factor_panels, block_rows, couplings)


def solution(mesh):
    return jax.shard_map(
        on_device,
        mesh=mesh,
        in_specs=(P("row", "col"), P(None, "row", "col"), P(), P()),
        out_specs=P(None, ("row", "col"), None),
        check_vma=False,
    )
```

```python
import functools

import jax
import jax.numpy as jnp
from jax import lax
from jax.experimental import pallas as pl
from jax.experimental.pallas import tpu as pltpu
from jax.sharding import PartitionSpec as P


LANES = 128
CORES = 2
REPLICA_BYTES = 4 << 20
KERNEL_BYTES = 12 << 20
ANY = pl.BlockSpec(memory_space=pl.ANY)
VMEM = pl.BlockSpec(memory_space=pltpu.VMEM)
SMEM = pl.BlockSpec(memory_space=pltpu.SMEM)


def streamed(inverse_tiles, factor_panels, block_rows, couplings):
    _, tile_cols = inverse_tiles.shape
    piece_rows = factor_panels.shape[1]
    listed = block_rows.shape[1]
    col_count = lax.axis_size("col")
    block_size = factor_panels.shape[2] * col_count // listed
    local_blocks = tile_cols // block_size
    my_column = lax.axis_index("col")
    offset = my_column * local_blocks
    targets = offset + jnp.arange(local_blocks, dtype=jnp.int32)
    results = []
    previous = None
    for section in range(factor_panels.shape[0]):
        section_rows = block_rows[section]
        gathered = lax.all_gather(factor_panels[section], "col", axis=1, tiled=True)
        onehot = (section_rows[:, None] == targets[None, :]).astype(jnp.float32)
        picked = jnp.einsum(
            "wpr,pq->wqr",
            gathered.reshape(piece_rows, listed, block_size),
            onehot,
            precision=lax.Precision.HIGHEST,
        ).reshape(piece_rows, tile_cols)
        partial_value = lax.dot_general(
            inverse_tiles,
            lax.all_gather(picked, "row", axis=0, tiled=True),
            (((1,), (1,)), ((), ())),
            precision=lax.Precision.HIGHEST,
            preferred_element_type=jnp.float32,
        )
        summed = lax.psum_scatter(partial_value, "col", scatter_dimension=0, tiled=True)
        if previous is not None:
            summed = summed + jnp.dot(
                previous,
                couplings[section - 1],
                precision=lax.Precision.HIGHEST,
                preferred_element_type=jnp.float32,
            )
        previous = -summed
        results.append(previous)
    return jnp.stack(results)


def call(kernel, out_shape, specs, scratch=()):
    run = pl.pallas_call(
        kernel,
        out_shape=out_shape,
        in_specs=specs,
        out_specs=jax.tree.map(lambda _: VMEM, out_shape),
        scratch_shapes=scratch,
        compiler_params=pltpu.CompilerParams(vmem_limit_bytes=KERNEL_BYTES),
    )
    return run


def split(value):
    high = value.astype(jnp.bfloat16)
    return high, (value - high.astype(jnp.float32)).astype(jnp.bfloat16)


def swap(value, axis, distances):
    pairs = [(i, i ^ distances[i % len(distances)]) for i in range(lax.axis_size(axis))]
    return lax.ppermute(value, axis, pairs)


def shift(value, axis, distance):
    count = lax.axis_size(axis)
    return lax.ppermute(value, axis, [(i, (i + distance) % count) for i in range(count)])


def pack_kernel(rows, fold, tile_hbm, panel_hbm, *refs):
    *outs, tile, panel, tile_done, panel_done = refs
    column = lax.axis_index("col")
    tile_copy = pltpu.make_async_copy(tile_hbm, tile, tile_done)
    panel_copy = pltpu.make_async_copy(panel_hbm, panel, panel_done)
    panel_copy.start()
    tile_copy.start()
    high = panel.shape[1] // fold
    tile_copy.wait()
    for away, out in enumerate(outs):
        start = pl.multiple_of(lax.rem(column + away, len(outs)) * rows, rows)
        out[panel.shape[0] * high :, :] = tile[pl.ds(start, rows), :]
    panel_copy.wait()
    for section in range(panel.shape[0]):
        dense = jnp.concatenate(
            [panel[section, i * high : (i + 1) * high, :] for i in range(fold)], axis=1
        )
        for out in outs:
            out[section * high : (section + 1) * high, :] = dense


def join_kernel(*refs):
    *parts, inverse, line = refs
    depth = line.shape[0] // len(parts)
    for away, part in enumerate(parts):
        inverse[:, away * LANES : (away + 1) * LANES] = part[depth:, :]
        line[away * depth : (away + 1) * depth, :] = part[:depth, :]


def both_kernel(own, other, out):
    rows = own.shape[0]
    core = lax.rem(lax.axis_index("row"), CORES)
    out[pl.ds(pl.multiple_of(core * rows, rows), rows), :] = own[...]
    out[pl.ds(pl.multiple_of((CORES - 1 - core) * rows, rows), rows), :] = other[...]


def chains(sections):
    return [(first, last) for last in range(1, sections) for first in reversed(range(last))]


def couplings_kernel(couplings, high_ref, low_ref):
    order = chains(couplings.shape[0] + 1)
    for at, (first, last) in enumerate(order):
        if first == last - 1:
            value = couplings[first]
        else:
            stacked = jnp.concatenate(split(couplings[first]), axis=0)
            after = order.index((first + 1, last))
            value = product(stacked, high_ref[after], low_ref[after])
        high_ref[at], low_ref[at] = split(value)


def place_kernel(fold, blocks_here, listed_here, block_size, block_rows, own_ref, other_ref, high_ref, low_ref):
    column = lax.axis_index("col")
    core = lax.rem(lax.axis_index("row"), CORES)
    sections = block_rows.shape[0]
    cols = high_ref.shape[0] // LANES
    width = listed_here * block_size
    depth = own_ref.shape[0] // cols // sections
    high_ref[...] = jnp.zeros_like(high_ref)
    low_ref[...] = jnp.zeros_like(low_ref)
    for section in range(sections):
        for first in range(0, cols, fold):
            pieces = []
            for e in range(CORES):
                parts = []
                for away in range(first, first + fold):
                    at = (away * sections + section) * depth
                    own, other = own_ref[at : at + depth, :], other_ref[at : at + depth, :]
                    parts.append(jnp.where(core == e, own, other))
                for i in range(fold):
                    pieces.append(
                        jnp.concatenate([part[:, i * width : (i + 1) * width] for part in parts], axis=1)
                    )
            high, low = split(jnp.concatenate(pieces, axis=0).T)
            for place in range(fold):
                for block in range(listed_here):
                    source = lax.rem(column + cols - (first + place), cols)
                    row = block_rows[section, source * listed_here + block]
                    tile = lax.rem(column + cols - row // blocks_here, cols)
                    start = tile * LANES + (row % blocks_here) * block_size
                    target = pl.ds(pl.multiple_of(start, block_size), block_size)
                    at = place * width + block * block_size
                    lanes = slice(section * LANES, (section + 1) * LANES)
                    high_ref[target, lanes] = high[at : at + block_size]
                    low_ref[target, lanes] = low[at : at + block_size]


def product(stacked, high, low):
    half = stacked.shape[0] // 2
    first = jnp.dot(stacked, high, preferred_element_type=jnp.float32)
    second = jnp.dot(stacked, low, preferred_element_type=jnp.float32)
    total = first + second
    return total[:half] + total[half:]


def multiply_kernel(*refs):
    half = (len(refs) - 2) // 2
    inverses, (high_ref, low_ref), outs = refs[:half], refs[half : half + 2], refs[half + 2 :]
    rows = inverses[0].shape[0]
    stacked = jnp.concatenate(split(jnp.concatenate([ref[...] for ref in inverses], axis=0)), axis=0)
    total = product(stacked, high_ref[...], low_ref[...])
    sections = total.shape[1] // LANES
    start = 0
    for out in outs:
        for at in range(0, out.shape[0], rows):
            section = at // rows % sections
            out[at : at + rows, :] = total[start : start + rows, section * LANES : (section + 1) * LANES]
            if section == sections - 1:
                start += rows


def other_kernel(pair, out):
    size = out.shape[0]
    core = lax.rem(lax.axis_index("row"), CORES)
    out[...] = pair[pl.ds(pl.multiple_of((CORES - 1 - core) * size, size), size), :]


def chained(values, high_ref, low_ref, blocks):
    def rows(ref, at):
        return jnp.concatenate([ref[at, block, :] for block in blocks], axis=0)

    order = chains(len(values))
    stacks = [jnp.concatenate(split(value), axis=0) for value in values]
    totals = []
    for last in range(len(values)):
        total = None
        for first in range(last):
            at = order.index((first, last))
            term = product(stacks[first], rows(high_ref, at), rows(low_ref, at))
            term = term if (last - first) % 2 else -term
            total = term if total is None else total + term
        totals.append(total)
    return totals


def blocks_of(*distances):
    chip = lax.div(lax.axis_index("row"), CORES)
    return [pl.ds(pl.multiple_of((chip ^ away) * LANES, LANES), LANES) for away in distances]


def advance(start, parts, blocks, high_ref, low_ref, out):
    sections, rows, _ = out.shape
    values = [
        [part[section * rows : (section + 1) * rows, :] for part in parts] for section in range(sections)
    ]
    totals = chained([jnp.concatenate(value, axis=1) for value in values], high_ref, low_ref, blocks)
    for section, total in enumerate(totals):
        base = jnp.zeros(out.shape[1:], jnp.float32) if start is None else start[section]
        out[section] = base if total is None else base + total
        for block, value in zip(blocks, values[section]):
            out[section, :, block] = out[section, :, block] - value


def partial_kernel(own, far, high_ref, low_ref, out):
    core = lax.rem(lax.axis_index("row"), CORES)
    size = own.shape[0]
    kept = far.at[pl.ds(pl.multiple_of(core * size, size), size), :]
    advance(None, [own, kept], blocks_of(0, jnp.where(core == 0, 1, 3)), high_ref, low_ref, out)


def finish_kernel(partial, near, handed, high_ref, low_ref, out):
    core = lax.rem(lax.axis_index("row"), CORES)
    advance(partial, [near, handed], blocks_of(2, jnp.where(core == 0, 3, 1)), high_ref, low_ref, out)


def gathered(inverse_tiles, factor_panels, block_rows, couplings):
    f32 = jnp.float32
    sections, piece_rows, width = factor_panels.shape
    count, cols = lax.axis_size("row"), lax.axis_size("col")
    listed = block_rows.shape[1]
    block_size = width * cols // listed
    fold = LANES // width
    rows = inverse_tiles.shape[0] // cols
    order = inverse_tiles.shape[1] * cols
    depth = sections * piece_rows // fold

    bf16 = jnp.bfloat16
    beside, along, across = ([CORES * i] for i in (1, 2, 3))
    pair, far = [1], beside + across

    packed = call(
        functools.partial(pack_kernel, rows, fold),
        [jax.ShapeDtypeStruct((depth + rows, LANES), f32)] * cols,
        [ANY, ANY],
        [
            pltpu.VMEM(inverse_tiles.shape, f32),
            pltpu.VMEM(factor_panels.shape, f32),
            pltpu.SemaphoreType.DMA,
            pltpu.SemaphoreType.DMA,
        ],
    )(*[pltpu.with_memory_space_constraint(x, pltpu.HBM) for x in (inverse_tiles, factor_panels)])
    arrived = [packed[0]] + [shift(packed[away], "col", away) for away in range(1, cols)]
    inverse, line = call(
        join_kernel,
        [jax.ShapeDtypeStruct((rows, order), f32), jax.ShapeDtypeStruct((cols * depth, LANES), f32)],
        [VMEM] * cols,
    )(*arrived)
    other, other_line = swap(inverse, "row", pair), swap(line, "row", pair)
    both = call(both_kernel, jax.ShapeDtypeStruct((CORES * rows, order), f32), [VMEM, VMEM])(inverse, other)
    inverses = [inverse, swap(inverse, "row", along), swap(both, "row", far)]
    placed = call(
        functools.partial(place_kernel, fold, LANES // block_size, listed // cols, block_size),
        [jax.ShapeDtypeStruct((order, sections * LANES), bf16)] * 2,
        [SMEM, VMEM, VMEM],
    )(block_rows, line, other_line)
    own, to_near, to_far = call(
        multiply_kernel,
        [jax.ShapeDtypeStruct((n * sections * rows, LANES), f32) for n in (1, 1, CORES)],
        [VMEM] * (len(inverses) + 2),
    )(*inverses, *placed)
    from_far = swap(to_far, "row", far)
    from_near = swap(to_near, "row", along)
    handed = swap(
        call(other_kernel, jax.ShapeDtypeStruct((sections * rows, LANES), f32), [VMEM])(from_far), "row", pair
    )
    halves = call(
        couplings_kernel, [jax.ShapeDtypeStruct((len(chains(sections)),) + couplings.shape[1:], bf16)] * 2, [VMEM]
    )(couplings)
    result = jax.ShapeDtypeStruct((sections, rows, piece_rows * count), f32)
    partial = call(partial_kernel, result, [VMEM] * 4)(own, from_far, *halves)
    return call(finish_kernel, result, [VMEM] * 5)(partial, from_near, handed, *halves)


def on_device(inverse_tiles, factor_panels, block_rows, couplings):
    sections, piece_rows, width = factor_panels.shape
    count, cols = lax.axis_size("row"), lax.axis_size("col")
    powers = all(n & (n - 1) == 0 for n in (count, cols))
    fits = sections * piece_rows * width * count * cols * 4 <= REPLICA_BYTES
    lanes = inverse_tiles.shape[1] == LANES == CORES * piece_rows and LANES % width == 0
    square = count == 4 * CORES
    if powers and fits and lanes and square and cols % (LANES // width) == 0:
        return gathered(inverse_tiles, factor_panels, block_rows, couplings)
    return streamed(inverse_tiles, factor_panels, block_rows, couplings)


def solution(mesh):
    return jax.shard_map(
        on_device,
        mesh=mesh,
        in_specs=(P("row", "col"), P(None, "row", "col"), P(), P()),
        out_specs=P(None, ("row", "col"), None),
        check_vma=False,
    )
```
